32 devices in a mesh: dp: 2 (over core), seq: 4 (over z), head: 4 (over y, x).
Axes of the slice: x: 2, y: 2, z: 4, core: 2. Of those that a mesh axis runs over, the one named last changes fastest.
Arguments:
- x_in: bfloat16 [2, 2048, 8192], P('dp', 'seq', 'head'), may hold values from -6 to 6
- b_in: bfloat16 [2, 2048, 128], P('dp', 'seq'), may hold values from -0.06591797 to 0.06591797
- c_in: bfloat16 [2, 2048, 128], P('dp', 'seq'), may hold values from -6 to 6
- rates: float32 [2, 128, 2048], P('dp', 'head', 'seq'), may hold values from 0 to 1, as said below
- skip: float32 [128], P('head'), may hold values from 0.1 to 1.9
- doc_lengths: int32 [2, 8], P('dp'), may hold values from 1 to 1536, 2048 in all within a row
- grad_y: bfloat16 [2, 2048, 8192], P('dp', ('seq', 'head')), may hold values from -6 to 6
Outputs:
- y_out: bfloat16 [2, 2048, 8192], P('dp', 'seq', 'head')
- grad_x: bfloat16 [2, 2048, 8192], P('dp', 'seq', 'head')
- grad_skip: float32 [128], P('head')
The draws below stay inside these ranges and needn't reach their ends.
Inputs may be any that keep to these rules, and one draw needn't show every extreme that they name: rates are positive. `doc_lengths`: each row sums to 2048, and its largest entry is exactly 1536.
All inputs are finite; a program needn't handle non-finite values.
Results may differ from the reference program's by a relative error of at most 0.0024.
Values may be sent and summed in bfloat16 or wider, within the bound.
A program may use at most 128 MiB of HBM per device.

```python
import math
import jax
import jax.numpy as jnp
import numpy as np
from jax import lax

HEADS = 128
HEAD_DIM = 64
STATE = 128
GROUP = 128
DOCS = 8
TOK_DEV = 512
PACKED_BATCH = 2
PACKED_LENGTH = 2048


def draw_rates(key, part):
    key_base, key_factor, random_key_location, key_amount = jax.random.split(jax.random.fold_in(key, 17), 4)
    minimum_value = 0.1 / PACKED_LENGTH
    highest = 0.03
    spread = jax.random.uniform(key_base, (PACKED_BATCH, HEADS, 1), jnp.float32)
    base = jnp.exp(jnp.log(minimum_value) + spread * (jnp.log(highest) - jnp.log(minimum_value)))
    factor = jnp.exp(jax.random.uniform(key_factor, (PACKED_BATCH, HEADS, PACKED_LENGTH), jnp.float32, jnp.log(0.5), jnp.log(2.0)))
    break_location = jax.random.randint(random_key_location, (PACKED_BATCH, 4), 0, PACKED_LENGTH)
    token_positions = jnp.arange(PACKED_LENGTH)
    document_break = jnp.any(token_positions[None, :, None] == break_location[:, None, :], axis=-1)
    amount = jax.random.uniform(key_amount, (PACKED_BATCH, 1, PACKED_LENGTH), jnp.float32, 0.22, 0.7)
    return (base * factor + jnp.where(document_break[:, None, :], amount, 0.0)).astype(jnp.float32)


def steps_of(stream_key, dims, cuts, smallest, largest):
    gain, own = 1.0, jax.random.fold_in(stream_key, 6)
    for position, parts in cuts:
        draws = jnp.exp(jax.random.uniform(jax.random.fold_in(own, position), (parts,), jnp.float32, smallest / len(cuts), largest / len(cuts)))
        gain = gain * jnp.repeat(draws, dims[position] // parts).reshape([-1 if axis == position else 1 for axis in range(len(dims))])
    return gain


def profile(count, total, reach, lean):
    loads = [(1 << 20) // math.isqrt(standing ** lean) + 1 for standing in range(2, count + 1)]
    rest, holding = total - reach - (count - 1), [1] * (count - 1)
    while rest > 0:
        movable = [i for i in range(count - 1) if holding[i] < reach]
        mass, budget = sum([loads[i] for i in movable]), rest
        for i in movable:
            addition = min(reach - holding[i], max(1, budget * loads[i] // mass), rest)
            holding[i] = holding[i] + addition
            rest = rest - addition
    return np.array([reach] + holding)


def uneven(stream_key, count, total, most, lean):
    if count == 2:
        one = jax.random.randint(stream_key, (), max(1, total - most), min(most, total - 1) + 1)
        return jnp.stack([one, total - one])
    tallies = jnp.asarray(profile(count, total, most, lean), jnp.int32)
    couples = (count - 1) // 2
    donor, taker = tallies[1:1 + 2 * couples:2], tallies[2:2 + 2 * couples:2]
    margin = jnp.minimum(donor - 1, most - taker)
    passed = jax.random.randint(jax.random.fold_in(stream_key, 1), (couples,), 0, 1 << 20) % (margin + 1)
    tallies = tallies.at[1:1 + 2 * couples:2].set(donor - passed).at[2:2 + 2 * couples:2].set(taker + passed)
    return tallies[jax.random.permutation(jax.random.fold_in(stream_key, 2), count)]


def centred(rng, dims, deviation, limit, cuts=(), kind=jnp.bfloat16):
    drawn = deviation * jax.random.normal(rng, dims, jnp.float32)
    if cuts:
        drawn = drawn * steps_of(rng, dims, cuts, -0.22, 0.18)
    return jnp.clip(drawn, -limit, limit).astype(kind)


def setup_inputs(seed: int = 0) -> dict:
    key_of = jax.random.split(jax.random.key(seed), 8)
    x_in = centred(key_of[0], (PACKED_BATCH, PACKED_LENGTH, HEADS * HEAD_DIM), 1.0, 6.0, ((0, 2), (1, 4), (2, 4)))
    b_in = centred(key_of[1], (PACKED_BATCH, PACKED_LENGTH, STATE), (0.125 / STATE ** 0.5), 0.06591797, ((0, 2), (1, 4)))
    c_in = centred(key_of[2], (PACKED_BATCH, PACKED_LENGTH, STATE), 1.0, 6.0, ((0, 2), (1, 4)))
    rates = draw_rates(jax.random.fold_in(key_of[7], 71), 0)
    skip = jnp.clip(1.0 + 0.18 * jax.random.normal(key_of[4], (HEADS,), jnp.float32), 0.1, 1.9)
    doc_lengths = jax.vmap(lambda own: uneven(own, DOCS, PACKED_LENGTH, 3 * TOK_DEV, 2))(jax.random.split(key_of[5], PACKED_BATCH)).reshape((PACKED_BATCH, DOCS)).astype(jnp.int32)
    grad_y = centred(key_of[6], (PACKED_BATCH, PACKED_LENGTH, HEADS * HEAD_DIM), 1.0, 6.0, ((0, 2), (1, 16)))
    return {"x_in": x_in, "b_in": b_in, "c_in": c_in, "rates": rates, "skip": skip, "doc_lengths": doc_lengths, "grad_y": grad_y}


def block_terms(b_rows, c_rows, rate_rows, doc_rows, prev_doc):
    running = jnp.cumsum(rate_rows, axis=1)
    inner = jnp.dot(c_rows, b_rows.T, preferred_element_type=jnp.float32)
    order = jnp.arange(doc_rows.shape[0], dtype=jnp.int32)
    same_doc = (doc_rows[:, None] == doc_rows[None, :]) & (order[:, None] >= order[None, :])
    gaps = running[:, :, None] - running[:, None, :]
    weights = jnp.exp(-jnp.where(same_doc[None], gaps, 1e+30))
    scores = (weights * inner[None]).astype(jnp.bfloat16)
    to_end = jnp.where((doc_rows == doc_rows[-1])[None], jnp.exp(-(running[:, -1:] - running)), 0.0)
    from_prev = jnp.where((doc_rows == prev_doc)[None], jnp.exp(-running), 0.0)
    return (scores, to_end, from_prev)

def forward_block(carried_state, inputs_block):
    x_rows, b_rows, c_rows, scores, to_end, from_prev, end_prev = inputs_block
    inside = jnp.einsum('hts,shp->thp', scores.astype(jnp.float32), x_rows.astype(jnp.float32))
    carried = from_prev.T[:, :, None] * jnp.einsum('tn,hnp->thp', c_rows.astype(jnp.float32), carried_state, precision=lax.Precision.HIGHEST)
    weighted = to_end[:, :, None] * b_rows.astype(jnp.float32)[None]
    updated = end_prev[:, None, None] * carried_state + jnp.einsum('hsn,shp->hnp', weighted, x_rows.astype(jnp.float32), precision=lax.Precision.HIGHEST)
    return (updated, inside + carried)

def backward_block(adjoint, inputs_block):
    g_rows, b_rows, c_rows, scores, to_end, from_prev, end_prev = inputs_block
    inside = jnp.einsum('hts,thp->shp', scores.astype(jnp.float32), g_rows.astype(jnp.float32))
    carried = to_end.T[:, :, None] * jnp.einsum('sn,hnp->shp', b_rows.astype(jnp.float32), adjoint, precision=lax.Precision.HIGHEST)
    weighted = from_prev[:, :, None] * c_rows.astype(jnp.float32)[None]
    updated = end_prev[:, None, None] * adjoint + jnp.einsum('htn,thp->hnp', weighted, g_rows.astype(jnp.float32), precision=lax.Precision.HIGHEST)
    return (updated, inside + carried)

def local_sweeps(x_heads, grad_heads, b_rows, c_rows, rate_rows, doc_rows, prev_doc):
    row_count, heads_local, head_dim = x_heads.shape
    block_count = row_count // GROUP
    state_dim = b_rows.shape[1]
    blocks_x = x_heads.reshape(block_count, GROUP, heads_local, head_dim)
    blocks_g = grad_heads.reshape(block_count, GROUP, heads_local, head_dim)
    blocks_b = b_rows.reshape(block_count, GROUP, state_dim)
    blocks_c = c_rows.reshape(block_count, GROUP, state_dim)
    blocks_rate = rate_rows.reshape(heads_local, block_count, GROUP).transpose(1, 0, 2)
    blocks_doc = doc_rows.reshape(block_count, GROUP)
    prev_docs = jnp.concatenate([prev_doc[None], blocks_doc[:-1, -1]]).astype(jnp.int32)
    scores, to_end, from_prev = jax.vmap(block_terms)(blocks_b, blocks_c, blocks_rate, blocks_doc, prev_docs)
    end_prev = from_prev[:, :, -1]
    zero_state = jnp.zeros((heads_local, state_dim, head_dim), jnp.float32)
    states_end, forward_out = lax.scan(forward_block, zero_state, (blocks_x, blocks_b, blocks_c, scores, to_end, from_prev, end_prev))
    final_adjoint, backward_out = lax.scan(backward_block, zero_state, (blocks_g, blocks_b, blocks_c, scores, to_end, from_prev, end_prev), reverse=True)
    shape_out = (row_count, heads_local, head_dim)
    return (forward_out.reshape(shape_out), states_end, backward_out.reshape(shape_out), final_adjoint)

def reference(x_in, b_in, c_in, rates, skip, doc_lengths, grad_y):

    def single_sequence(inputs_seq):
        x_rows, b_rows, c_rows, rate_rows, lengths, g_rows = inputs_seq
        seq_length = x_rows.shape[0]
        token_positions = jnp.arange(seq_length, dtype=jnp.int32)
        doc_ends = jnp.cumsum(lengths)[:-1]
        documents = lax.optimization_barrier(jnp.sum((token_positions[:, None] >= doc_ends[None, :]).astype(jnp.int32), axis=1)).astype(jnp.int32)
        x_heads = x_rows.reshape(seq_length, HEADS, HEAD_DIM)
        grad_heads = g_rows.reshape(seq_length, HEADS, HEAD_DIM)
        forward_out, states_end, backward_out, final_adjoint = local_sweeps(x_heads, grad_heads, b_rows, c_rows, rate_rows, documents, jnp.int32(-1))
        skip_gain = skip[None, :, None]
        out_values = (forward_out + skip_gain * x_heads.astype(jnp.float32)).astype(jnp.bfloat16).reshape(seq_length, -1)
        grad_values = (backward_out + skip_gain * grad_heads.astype(jnp.float32)).astype(jnp.bfloat16).reshape(seq_length, -1)
        partial_value = lax.optimization_barrier(jnp.sum(x_heads.astype(jnp.float32) * grad_heads.astype(jnp.float32), axis=(0, 2)))
        return (out_values, grad_values, partial_value)
    out_values, grad_values, per_sequence = lax.map(single_sequence, (x_in, b_in, c_in, rates, doc_lengths, grad_y))
    grad_skip = lax.optimization_barrier(jnp.sum(per_sequence, axis=0)) / jnp.sqrt(jnp.float32(PACKED_BATCH * PACKED_LENGTH * HEAD_DIM))
    return (out_values, grad_values, grad_skip)
```

```python
import functools
import math

import jax
import jax.numpy as jnp
from jax import lax
from jax.experimental import pallas as pl
from jax.experimental.pallas import tpu as pltpu
from jax.sharding import PartitionSpec as P

HEAD_DIM = 64
GROUP = 128
LANES = 128
PAIR = LANES // HEAD_DIM
EXACT = lax.Precision.HIGHEST
F32 = jnp.float32
BF16 = jnp.bfloat16


def split(value, axis):
    high = value.astype(BF16)
    low = (value - high.astype(F32)).astype(BF16)
    return jnp.concatenate([high, low], axis=axis)


def dot(a, b):
    return jnp.dot(a, b, preferred_element_type=F32)


def tdot(a, b):
    return lax.dot_general(a, b, (((0,), (0,)), ((), ())), preferred_element_type=F32)


def ndot(a, b):
    return lax.dot_general(a, b, (((1,), (1,)), ((), ())), preferred_element_type=F32)


def iota(axis):
    return lax.broadcasted_iota(jnp.int32, (GROUP, GROUP), axis)


def doc_of(position, ends):
    return sum((position >= end).astype(jnp.int32) for end in ends)


def doc_ends(lengths_ref):
    ends = []
    total = jnp.int32(0)
    for k in range(lengths_ref.shape[1] - 1):
        total = total + lengths_ref[0, k]
        ends.append(total)
    return ends


def block_masks(ends, first):
    here = doc_of(first + iota(0), ends)
    prev = doc_of(jnp.full((GROUP, GROUP), first - 1, jnp.int32), ends)
    last = doc_of(jnp.full((GROUP, GROUP), first + GROUP - 1, jnp.int32), ends)
    return here, (here == prev).astype(F32), (here == last).astype(F32)


def running_columns(rates, lower):
    return lax.dot_general(
        lower, rates, (((1,), (1,)), ((), ())), precision=EXACT, preferred_element_type=F32
    )


def pair_columns(columns, pair):
    wide = [
        jnp.broadcast_to(columns[:, h : h + 1], (GROUP, GROUP))
        for h in range(pair * PAIR, pair * PAIR + PAIR)
    ]
    lane_head = iota(1) // HEAD_DIM
    joined = wide[0]
    for h in range(1, PAIR):
        joined = jnp.where(lane_head == h, wide[h], joined)
    return wide, joined


def states_kernel(pairs, lengths_ref, x_ref, g_ref, b_ref, c_ref, rates_ref,
                  state_ref, adjoint_ref, decay_ref, partial_ref,
                  from_mask, to_mask, b_t, c_t):
    rows = x_ref.shape[0]
    blocks = rows // GROUP

    @pl.when(pl.program_id(0) == 0)
    def _():
        ends = doc_ends(lengths_ref)
        start = lax.axis_index("seq") * rows
        for k in range(blocks):
            span = slice(k * GROUP, (k + 1) * GROUP)
            _, from_mask[k], to_mask[k] = block_masks(ends, start + k * GROUP)
            bt = b_ref[span].astype(F32).T.astype(BF16)
            ct = c_ref[span].astype(F32).T.astype(BF16)
            b_t[k] = jnp.concatenate([bt, bt], axis=1)
            c_t[k] = jnp.concatenate([ct, ct], axis=1)

    lower = (iota(1) <= iota(0)).astype(F32)
    columns = [
        running_columns(rates_ref[0, :, k * GROUP : (k + 1) * GROUP], lower) for k in range(blocks)
    ]
    for pair in range(pairs):
        lanes = slice(pair * LANES, (pair + 1) * LANES)
        state = jnp.zeros((b_ref.shape[1], LANES), F32)
        adjoint = jnp.zeros_like(state)
        decay = jnp.ones((1, LANES), F32)
        partial = jnp.zeros((GROUP, LANES), F32)
        leaving = []
        for k in range(blocks):
            span = slice(k * GROUP, (k + 1) * GROUP)
            _, run = pair_columns(columns[k], pair)
            come = jnp.exp(-run) * from_mask[k]
            go = jnp.exp(run - run[GROUP - 1 : GROUP]) * to_mask[k]
            end = come[GROUP - 1 : GROUP]
            x = x_ref[span, lanes].astype(F32)
            g = g_ref[span, lanes].astype(F32)
            partial = partial + x * g
            state = end * state + dot(b_t[k], split(go * x, 0))
            decay = decay * end
            leaving.append((end, dot(c_t[k], split(come * g, 0))))
        for end, add in reversed(leaving):
            adjoint = end * adjoint + add
        state_ref[pair] = state
        adjoint_ref[pair] = adjoint
        decay_ref[pair] = decay
        partial_ref[pair] = jnp.sum(partial, axis=0, keepdims=True)


def chain_kernel(state_ref, adjoint_ref, decay_ref, into_ref, back_ref,
                 state_out, adjoint_out, send_f, recv_f, send_b, recv_b):
    count = lax.axis_size("seq")
    me = lax.axis_index("seq")
    later = jnp.minimum(me + 1, count - 1)
    earlier = jnp.maximum(me - 1, 0)
    first, last = me == 0, me == count - 1
    mesh_id = pl.DeviceIdType.MESH
    barrier = pltpu.get_barrier_semaphore()

    @pl.when(jnp.logical_not(first))
    def _():
        pl.semaphore_signal(barrier, inc=1, device_id={"seq": earlier}, device_id_type=mesh_id)

    @pl.when(jnp.logical_not(last))
    def _():
        pl.semaphore_signal(barrier, inc=1, device_id={"seq": later}, device_id_type=mesh_id)

    pl.semaphore_wait(
        barrier, jnp.where(first, 0, 1).astype(jnp.int32) + jnp.where(last, 0, 1).astype(jnp.int32)
    )

    def forward(q):
        return pltpu.make_async_remote_copy(
            src_ref=state_out.at[q], dst_ref=into_ref.at[q], send_sem=send_f.at[q],
            recv_sem=recv_f.at[q], device_id={"seq": later}, device_id_type=mesh_id)

    def backward(q):
        return pltpu.make_async_remote_copy(
            src_ref=adjoint_out.at[q], dst_ref=back_ref.at[q], send_sem=send_b.at[q],
            recv_sem=recv_b.at[q], device_id={"seq": earlier}, device_id_type=mesh_id)

    @pl.loop(0, state_ref.shape[0])
    def _(q):
        @pl.when(first)
        def _():
            into_ref[q] = jnp.zeros_like(into_ref[q])
            state_out[q] = state_ref[q]
            forward(q).start()

        @pl.when(jnp.logical_not(first) & jnp.logical_not(last))
        def _():
            forward(q).wait_recv()
            state_out[q] = decay_ref[q] * into_ref[q] + state_ref[q]
            forward(q).start()

        @pl.when(last)
        def _():
            back_ref[q] = jnp.zeros_like(back_ref[q])
            adjoint_out[q] = adjoint_ref[q]
            backward(q).start()

        @pl.when(jnp.logical_not(first) & jnp.logical_not(last))
        def _():
            backward(q).wait_recv()
            adjoint_out[q] = decay_ref[q] * back_ref[q] + adjoint_ref[q]
            backward(q).start()

    @pl.loop(0, state_ref.shape[0])
    def _(q):
        @pl.when(last)
        def _():
            forward(q).wait_recv()

        @pl.when(first)
        def _():
            backward(q).wait_recv()

        @pl.when(jnp.logical_not(last))
        def _():
            forward(q).wait_send()

        @pl.when(jnp.logical_not(first))
        def _():
            backward(q).wait_send()


def final_kernel(pairs, lengths_ref, x_ref, g_ref, b_ref, c_ref, rates_ref, skip_ref,
                 into_ref, back_ref, y_ref, gx_ref,
                 from_mask, to_mask, b_t, c_t, inner_ref):
    rows = x_ref.shape[0]
    blocks = rows // GROUP

    @pl.when(pl.program_id(0) == 0)
    def _():
        ends = doc_ends(lengths_ref)
        start = lax.axis_index("seq") * rows
        for k in range(blocks):
            span = slice(k * GROUP, (k + 1) * GROUP)
            at = start + k * GROUP
            here, from_mask[k], to_mask[k] = block_masks(ends, at)
            bt = b_ref[span].astype(F32).T.astype(BF16)
            ct = c_ref[span].astype(F32).T.astype(BF16)
            b_t[k] = jnp.concatenate([bt, bt], axis=1)
            c_t[k] = jnp.concatenate([ct, ct], axis=1)
            inner = ndot(c_ref[span], b_ref[span])
            same = (here == doc_of(at + iota(1), ends)) & (iota(0) >= iota(1))
            inner_ref[k] = jnp.where(same, inner, 0.0)

    lower = (iota(1) <= iota(0)).astype(F32)
    upper = (iota(0) <= iota(1)).astype(F32)
    lane_head = iota(1) // HEAD_DIM
    columns, lines = [], []
    for k in range(blocks):
        rates = rates_ref[0, :, k * GROUP : (k + 1) * GROUP]
        columns.append(running_columns(rates, lower))
        lines.append(jnp.dot(rates, upper, precision=EXACT, preferred_element_type=F32))

    def stack(value):
        zero = jnp.zeros_like(value)
        return jnp.concatenate([jnp.where(lane_head == h, value, zero) for h in range(PAIR)], axis=0)

    for pair in range(pairs):
        lanes = slice(pair * LANES, (pair + 1) * LANES)
        gain = skip_ref[pair]
        state = into_ref[pair]
        later = []
        for k in range(blocks):
            span = slice(k * GROUP, (k + 1) * GROUP)
            wide, run = pair_columns(columns[k], pair)
            come = jnp.exp(-run) * from_mask[k]
            go = jnp.exp(run - run[GROUP - 1 : GROUP]) * to_mask[k]
            end = come[GROUP - 1 : GROUP]
            inner = inner_ref[k]
            scores = [
                (jnp.exp(jnp.minimum(lines[k][pair * PAIR + h : pair * PAIR + h + 1] - wide[h], 0.0))
                 * inner).astype(BF16)
                for h in range(PAIR)
            ]
            x = x_ref[span, lanes]
            g = g_ref[span, lanes]
            xf = x.astype(F32)
            gf = g.astype(F32)
            c = c_ref[span]
            carried = come * dot(jnp.concatenate([c, c], axis=1), split(state, 0))
            inside = dot(jnp.concatenate(scores, axis=1), stack(x))
            y_ref[span, lanes] = (inside + carried + gain * xf).astype(BF16)
            if k + 1 < blocks:
                state = end * state + dot(b_t[k], split(go * xf, 0))
            back = tdot(jnp.concatenate(scores, axis=0), stack(g)) + gain * gf
            add = dot(c_t[k], split(come * gf, 0)) if k else None
            later.append((span, end, go, back, add))
        adjoint = back_ref[pair]
        for span, end, go, back, add in reversed(later):
            b = b_ref[span]
            carried = go * dot(jnp.concatenate([b, b], axis=1), split(adjoint, 0))
            gx_ref[span, lanes] = (back + carried).astype(BF16)
            if add is not None:
                adjoint = end * adjoint + add


def total_over(value, axis):
    count = lax.axis_size(axis)
    step = 1
    while step < count:
        other = lax.ppermute(value, axis, [(i, i ^ step) for i in range(count)])
        value = value + other
        step *= 2
    return value


def shards(x_in, b_in, c_in, rates, skip, doc_lengths, grad_y):
    _, rows, width = x_in.shape
    heads = skip.shape[0]
    state_dim = b_in.shape[2]
    all_pairs = width // LANES
    pairs = math.gcd(all_pairs, 2)
    steps = all_pairs // pairs
    blocks = rows // GROUP
    chunk = pairs * LANES

    grad_local = lax.all_to_all(grad_y, "head", split_axis=2, concat_axis=1, tiled=True)
    x, g, b, c = x_in[0], grad_local[0], b_in[0], c_in[0]
    rates_steps = rates.reshape(steps, pairs * PAIR, rows)
    gains = jnp.repeat(skip, HEAD_DIM).reshape(all_pairs, 1, LANES)

    wide = pl.BlockSpec((rows, chunk), lambda i: (0, i))
    whole = pl.BlockSpec((rows, state_dim), lambda i: (0, 0))
    lengths_spec = pl.BlockSpec(memory_space=pltpu.SMEM)
    rate_spec = pl.BlockSpec((1, pairs * PAIR, rows), lambda i: (i, 0, 0))
    state_spec = pl.BlockSpec((pairs, state_dim, LANES), lambda i: (i, 0, 0))
    line_spec = pl.BlockSpec((pairs, 1, LANES), lambda i: (i, 0, 0))
    state_shape = jax.ShapeDtypeStruct((all_pairs, state_dim, LANES), F32)
    line_shape = jax.ShapeDtypeStruct((all_pairs, 1, LANES), F32)
    setup = [
        pltpu.VMEM((blocks, GROUP, GROUP), F32),
        pltpu.VMEM((blocks, GROUP, GROUP), F32),
        pltpu.VMEM((blocks, state_dim, 2 * GROUP), BF16),
        pltpu.VMEM((blocks, state_dim, 2 * GROUP), BF16),
    ]

    states, adjoints, decays, partials = pl.pallas_call(
        functools.partial(states_kernel, pairs),
        grid=(steps,),
        in_specs=[lengths_spec, wide, wide, whole, whole, rate_spec],
        out_specs=[state_spec, state_spec, line_spec, line_spec],
        out_shape=[state_shape, state_shape, line_shape, line_shape],
        scratch_shapes=setup,
        name="states",
    )(doc_lengths, x, g, b, c, rates_steps)

    vmem = pl.BlockSpec(memory_space=pltpu.VMEM)
    into, back = pl.pallas_call(
        chain_kernel,
        in_specs=[vmem] * 3,
        out_specs=[vmem] * 2,
        out_shape=[state_shape] * 2,
        scratch_shapes=[
            pltpu.VMEM(state_shape.shape, F32),
            pltpu.VMEM(state_shape.shape, F32),
        ] + [pltpu.SemaphoreType.DMA((all_pairs,))] * 4,
        compiler_params=pltpu.CompilerParams(collective_id=0, has_side_effects=True),
        name="chain",
    )(states, adjoints, decays)

    sums = jnp.sum(partials.reshape(heads, HEAD_DIM), axis=1)
    sums = total_over(total_over(sums, "dp"), "seq")

    y, gx = pl.pallas_call(
        functools.partial(final_kernel, pairs),
        grid=(steps,),
        in_specs=[lengths_spec, wide, wide, whole, whole, rate_spec, line_spec, state_spec, state_spec],
        out_specs=[wide, wide],
        out_shape=[jax.ShapeDtypeStruct((rows, width), BF16)] * 2,
        scratch_shapes=setup + [pltpu.VMEM((blocks, GROUP, GROUP), F32)],
        cost_estimate=pl.CostEstimate(
            flops=24 * rows * GROUP * width, bytes_accessed=12 * rows * width, transcendentals=0
        ),
        name="final",
    )(doc_lengths, x, g, b, c, rates_steps, gains, into, back)

    tokens_all = lax.axis_size("dp") * lax.axis_size("seq") * rows * HEAD_DIM
    return y[None], gx[None], sums / math.sqrt(tokens_all)


def solution(mesh):
    placed = (
        P("dp", "seq", "head"),
        P("dp", "seq", None),
        P("dp", "seq", None),
        P("dp", "head", "seq"),
        P("head"),
        P("dp", None),
        P("dp", ("seq", "head"), None),
    )
    return jax.shard_map(
        shards,
        mesh=mesh,
        in_specs=placed,
        out_specs=(P("dp", "seq", "head"), P("dp", "seq", "head"), P("head")),
        check_vma=False,
    )
```

```python
import functools
import math

import jax
import jax.numpy as jnp
from jax import lax
from jax.experimental import pallas as pl
from jax.experimental.pallas import tpu as pltpu
from jax.sharding import PartitionSpec as P

HEAD_DIM = 64
GROUP = 128
LANES = 128
PAIR = LANES // HEAD_DIM
EXACT = lax.Precision.HIGHEST
F32 = jnp.float32
BF16 = jnp.bfloat16


def split(value, axis):
    high = value.astype(BF16)
    low = (value - high.astype(F32)).astype(BF16)
    return jnp.concatenate([high, low], axis=axis)


def dot(a, b):
    return jnp.dot(a, b, preferred_element_type=F32)


def tdot(a, b):
    return lax.dot_general(a, b, (((0,), (0,)), ((), ())), preferred_element_type=F32)


def ndot(a, b):
    return lax.dot_general(a, b, (((1,), (1,)), ((), ())), preferred_element_type=F32)


def iota(axis):
    return lax.broadcasted_iota(jnp.int32, (GROUP, GROUP), axis)


def doc_of(position, ends):
    return sum((position >= end).astype(jnp.int32) for end in ends)


def doc_ends(lengths_ref):
    ends = []
    total = jnp.int32(0)
    for k in range(lengths_ref.shape[1] - 1):
        total = total + lengths_ref[0, k]
        ends.append(total)
    return ends


def block_masks(ends, first):
    here = doc_of(first + iota(0), ends)
    prev = doc_of(jnp.full((GROUP, GROUP), first - 1, jnp.int32), ends)
    last = doc_of(jnp.full((GROUP, GROUP), first + GROUP - 1, jnp.int32), ends)
    return here, (here == prev).astype(F32), (here == last).astype(F32)


def running_columns(rates, lower):
    return lax.dot_general(
        lower, rates, (((1,), (1,)), ((), ())), precision=EXACT, preferred_element_type=F32
    )


def pair_columns(columns, pair):
    wide = [
        jnp.broadcast_to(columns[:, h : h + 1], (GROUP, GROUP))
        for h in range(pair * PAIR, pair * PAIR + PAIR)
    ]
    lane_head = iota(1) // HEAD_DIM
    joined = wide[0]
    for h in range(1, PAIR):
        joined = jnp.where(lane_head == h, wide[h], joined)
    return wide, joined


LAG = 2


def exchange_kernel(lengths_ref, x_ref, gy_ref, b_ref, c_ref, rates_ref,
                    g_ref, into_ref, back_ref, partial_ref,
                    state_out, adjoint_out, from_mask, to_mask, b_t, c_t,
                    send_f, recv_f, send_b, recv_b, send_g, recv_g, own_sem):
    rows, width = x_ref.shape
    blocks = rows // GROUP
    pair_count = width // LANES
    own_rows = gy_ref.shape[0]
    count, me = lax.axis_size("seq"), lax.axis_index("seq")
    head_count, head_me = lax.axis_size("head"), lax.axis_index("head")
    later = jnp.minimum(me + 1, count - 1)
    earlier = jnp.maximum(me - 1, 0)
    first, last = me == 0, me == count - 1
    mesh_id = pl.DeviceIdType.MESH

    own = pltpu.make_async_copy(
        gy_ref.at[:, pl.ds(pl.multiple_of(head_me * width, LANES), width)],
        g_ref.at[pl.ds(pl.multiple_of(head_me * own_rows, own_rows), own_rows)],
        own_sem,
    )
    own.start()
    barrier = pltpu.get_barrier_semaphore()

    @pl.when(jnp.logical_not(first))
    def _():
        pl.semaphore_signal(barrier, inc=1, device_id={"seq": earlier}, device_id_type=mesh_id)

    @pl.when(jnp.logical_not(last))
    def _():
        pl.semaphore_signal(barrier, inc=1, device_id={"seq": later}, device_id_type=mesh_id)

    @pl.loop(1, head_count)
    def _(i):
        pl.semaphore_signal(
            barrier, inc=1, device_id={"head": lax.rem(head_me + i, head_count)},
            device_id_type=mesh_id)

    pl.semaphore_wait(
        barrier, head_count - 1 + jnp.where(first, 0, 1).astype(jnp.int32)
        + jnp.where(last, 0, 1).astype(jnp.int32))

    def lanes_of(q):
        return pl.ds(pl.multiple_of(q * LANES, LANES), LANES)

    def cotangent(i, q):
        peer = lax.rem(head_me + i, head_count)
        return pltpu.make_async_remote_copy(
            src_ref=gy_ref.at[:, pl.ds(pl.multiple_of(peer * width + q * LANES, LANES), LANES)],
            dst_ref=g_ref.at[pl.ds(pl.multiple_of(head_me * own_rows, own_rows), own_rows), lanes_of(q)],
            send_sem=send_g.at[i - 1, q], recv_sem=recv_g.at[i - 1, q],
            device_id={"head": peer}, device_id_type=mesh_id)

    def forward(q):
        return pltpu.make_async_remote_copy(
            src_ref=state_out.at[q], dst_ref=into_ref.at[q], send_sem=send_f.at[q],
            recv_sem=recv_f.at[q], device_id={"seq": later}, device_id_type=mesh_id)

    def backward(q):
        return pltpu.make_async_remote_copy(
            src_ref=adjoint_out.at[q], dst_ref=back_ref.at[q], send_sem=send_b.at[q],
            recv_sem=recv_b.at[q], device_id={"seq": earlier}, device_id_type=mesh_id)

    @pl.loop(0, pair_count)
    def _(q):
        @pl.loop(1, head_count)
        def _(i):
            cotangent(i, q).start()

    ends = doc_ends(lengths_ref)
    for k in range(blocks):
        span = slice(k * GROUP, (k + 1) * GROUP)
        _, from_mask[k], to_mask[k] = block_masks(ends, me * rows + k * GROUP)
        bt = b_ref[span].astype(F32).T.astype(BF16)
        ct = c_ref[span].astype(F32).T.astype(BF16)
        b_t[k] = jnp.concatenate([bt, bt], axis=1)
        c_t[k] = jnp.concatenate([ct, ct], axis=1)
    own.wait()
    lower = (iota(1) <= iota(0)).astype(F32)

    def runs_of(q):
        runs = []
        for k in range(blocks):
            columns = running_columns(rates_ref[q, :, k * GROUP : (k + 1) * GROUP], lower)
            runs.append(pair_columns(columns, 0)[1])
        return runs

    def forward_step(q):
        state = jnp.zeros((b_ref.shape[1], LANES), F32)
        decay = jnp.ones((1, LANES), F32)
        for k, run in enumerate(runs_of(q)):
            total = run[GROUP - 1 : GROUP]
            go = jnp.exp(run - total) * to_mask[k]
            end = jnp.exp(-total) * from_mask[k, GROUP - 1 : GROUP]
            x = x_ref[k * GROUP : (k + 1) * GROUP, lanes_of(q)].astype(F32)
            state = end * state + dot(b_t[k], split(go * x, 0))
            decay = decay * end

        @pl.when(first)
        def _():
            into_ref[q] = jnp.zeros_like(state)
            state_out[q] = state
            forward(q).start()

        @pl.when(jnp.logical_not(first))
        def _():
            forward(q).wait_recv()

            @pl.when(jnp.logical_not(last))
            def _():
                state_out[q] = decay * into_ref[q] + state
                forward(q).start()

    def backward_step(q):
        @pl.loop(1, head_count)
        def _(i):
            cotangent(i, q).wait_recv()

        adjoint = jnp.zeros((b_ref.shape[1], LANES), F32)
        decay = jnp.ones((1, LANES), F32)
        partial = jnp.zeros((GROUP, LANES), F32)
        runs = runs_of(q)
        for k in reversed(range(blocks)):
            come = jnp.exp(-runs[k]) * from_mask[k]
            end = come[GROUP - 1 : GROUP]
            x = x_ref[k * GROUP : (k + 1) * GROUP, lanes_of(q)].astype(F32)
            g = g_ref[k * GROUP : (k + 1) * GROUP, lanes_of(q)].astype(F32)
            partial = partial + x * g
            adjoint = end * adjoint + dot(c_t[k], split(come * g, 0))
            decay = decay * end
        partial_ref[q] = jnp.sum(partial, axis=0, keepdims=True)

        @pl.when(last)
        def _():
            back_ref[q] = jnp.zeros_like(adjoint)
            adjoint_out[q] = adjoint
            backward(q).start()

        @pl.when(jnp.logical_not(last))
        def _():
            backward(q).wait_recv()

            @pl.when(jnp.logical_not(first))
            def _():
                adjoint_out[q] = decay * back_ref[q] + adjoint
                backward(q).start()

    @pl.loop(0, pair_count + LAG * (count - 1))
    def _(t):
        q = t - LAG * me
        r = t - LAG * (count - 1 - me)

        @pl.when((q >= 0) & (q < pair_count))
        def _():
            forward_step(q)

        @pl.when((r >= 0) & (r < pair_count))
        def _():
            backward_step(r)

    @pl.loop(0, pair_count)
    def _(q):
        @pl.loop(1, head_count)
        def _(i):
            cotangent(i, q).wait_send()

        @pl.when(jnp.logical_not(last))
        def _():
            forward(q).wait_send()

        @pl.when(jnp.logical_not(first))
        def _():
            backward(q).wait_send()


def final_kernel(pairs, lengths_ref, x_ref, g_ref, b_ref, c_ref, rates_ref, skip_ref,
                 into_ref, back_ref, y_ref, gx_ref,
                 from_mask, to_mask, b_t, c_t, inner_ref):
    rows = x_ref.shape[0]
    blocks = rows // GROUP

    @pl.when(pl.program_id(0) == 0)
    def _():
        ends = doc_ends(lengths_ref)
        start = lax.axis_index("seq") * rows
        for k in range(blocks):
            span = slice(k * GROUP, (k + 1) * GROUP)
            at = start + k * GROUP
            here, from_mask[k], to_mask[k] = block_masks(ends, at)
            bt = b_ref[span].astype(F32).T.astype(BF16)
            ct = c_ref[span].astype(F32).T.astype(BF16)
            b_t[k] = jnp.concatenate([bt, bt], axis=1)
            c_t[k] = jnp.concatenate([ct, ct], axis=1)
            inner = ndot(c_ref[span], b_ref[span])
            same = (here == doc_of(at + iota(1), ends)) & (iota(0) >= iota(1))
            inner_ref[k] = jnp.where(same, inner, 0.0)

    lower = (iota(1) <= iota(0)).astype(F32)
    upper = (iota(0) <= iota(1)).astype(F32)
    lane_head = iota(1) // HEAD_DIM
    columns, lines = [], []
    for k in range(blocks):
        rates = rates_ref[0, :, k * GROUP : (k + 1) * GROUP]
        columns.append(running_columns(rates, lower))
        lines.append(jnp.dot(rates, upper, precision=EXACT, preferred_element_type=F32))

    def stack(value):
        zero = jnp.zeros_like(value)
        return jnp.concatenate([jnp.where(lane_head == h, value, zero) for h in range(PAIR)], axis=0)

    for pair in range(pairs):
        lanes = slice(pair * LANES, (pair + 1) * LANES)
        gain = skip_ref[pair]
        state = into_ref[pair]
        later = []
        for k in range(blocks):
            span = slice(k * GROUP, (k + 1) * GROUP)
            wide, run = pair_columns(columns[k], pair)
            come = jnp.exp(-run) * from_mask[k]
            go = jnp.exp(run - run[GROUP - 1 : GROUP]) * to_mask[k]
            end = come[GROUP - 1 : GROUP]
            inner = inner_ref[k]
            scores = [
                (jnp.exp(jnp.minimum(lines[k][pair * PAIR + h : pair * PAIR + h + 1] - wide[h], 0.0))
                 * inner).astype(BF16)
                for h in range(PAIR)
            ]
            x = x_ref[span, lanes]
            g = g_ref[span, lanes]
            xf = x.astype(F32)
            gf = g.astype(F32)
            c = c_ref[span]
            carried = come * dot(jnp.concatenate([c, c], axis=1), split(state, 0))
            inside = dot(jnp.concatenate(scores, axis=1), stack(x))
            y_ref[span, lanes] = (inside + carried + gain * xf).astype(BF16)
            if k + 1 < blocks:
                state = end * state + dot(b_t[k], split(go * xf, 0))
            back = tdot(jnp.concatenate(scores, axis=0), stack(g)) + gain * gf
            add = dot(c_t[k], split(come * gf, 0)) if k else None
            later.append((span, end, go, back, add))
        adjoint = back_ref[pair]
        for span, end, go, back, add in reversed(later):
            b = b_ref[span]
            carried = go * dot(jnp.concatenate([b, b], axis=1), split(adjoint, 0))
            gx_ref[span, lanes] = (back + carried).astype(BF16)
            if add is not None:
                adjoint = end * adjoint + add


def total_over(value, axis):
    count = lax.axis_size(axis)
    step = 1
    while step < count:
        other = lax.ppermute(value, axis, [(i, i ^ step) for i in range(count)])
        value = value + other
        step *= 2
    return value


def shards(x_in, b_in, c_in, rates, skip, doc_lengths, grad_y):
    _, rows, width = x_in.shape
    heads = skip.shape[0]
    state_dim = b_in.shape[2]
    all_pairs = width // LANES
    pairs = math.gcd(all_pairs, 2)
    steps = all_pairs // pairs
    blocks = rows // GROUP
    chunk = pairs * LANES

    x, b, c = x_in[0], b_in[0], c_in[0]
    rates_steps = rates.reshape(steps, pairs * PAIR, rows)
    gains = jnp.repeat(skip, HEAD_DIM).reshape(all_pairs, 1, LANES)

    wide = pl.BlockSpec((rows, chunk), lambda i: (0, i))
    whole = pl.BlockSpec((rows, state_dim), lambda i: (0, 0))
    lengths_spec = pl.BlockSpec(memory_space=pltpu.SMEM)
    rate_spec = pl.BlockSpec((1, pairs * PAIR, rows), lambda i: (i, 0, 0))
    state_spec = pl.BlockSpec((pairs, state_dim, LANES), lambda i: (i, 0, 0))
    line_spec = pl.BlockSpec((pairs, 1, LANES), lambda i: (i, 0, 0))
    state_shape = jax.ShapeDtypeStruct((all_pairs, state_dim, LANES), F32)
    line_shape = jax.ShapeDtypeStruct((all_pairs, 1, LANES), F32)
    setup = [
        pltpu.VMEM((blocks, GROUP, GROUP), F32),
        pltpu.VMEM((blocks, GROUP, GROUP), F32),
        pltpu.VMEM((blocks, state_dim, 2 * GROUP), BF16),
        pltpu.VMEM((blocks, state_dim, 2 * GROUP), BF16),
    ]

    vmem = pl.BlockSpec(memory_space=pltpu.VMEM)
    peers = lax.axis_size("head") - 1
    dma = pltpu.SemaphoreType.DMA
    g, into, back, partials = pl.pallas_call(
        exchange_kernel,
        in_specs=[lengths_spec] + [vmem] * 5,
        out_specs=[vmem] * 4,
        out_shape=[jax.ShapeDtypeStruct((rows, width), BF16), state_shape, state_shape, line_shape],
        scratch_shapes=[pltpu.VMEM(state_shape.shape, F32)] * 2 + setup
        + [dma((all_pairs,))] * 4 + [dma((peers, all_pairs))] * 2 + [dma],
        compiler_params=pltpu.CompilerParams(collective_id=0, has_side_effects=True),
        name="exchange",
    )(doc_lengths, x, grad_y[0], b, c, rates.reshape(all_pairs, PAIR, rows))

    sums = jnp.sum(partials.reshape(heads, HEAD_DIM), axis=1)
    sums = total_over(total_over(sums, "dp"), "seq")

    y, gx = pl.pallas_call(
        functools.partial(final_kernel, pairs),
        grid=(steps,),
        in_specs=[lengths_spec, wide, wide, whole, whole, rate_spec, line_spec, state_spec, state_spec],
        out_specs=[wide, wide],
        out_shape=[jax.ShapeDtypeStruct((rows, width), BF16)] * 2,
        scratch_shapes=setup + [pltpu.VMEM((blocks, GROUP, GROUP), F32)],
        cost_estimate=pl.CostEstimate(
            flops=24 * rows * GROUP * width, bytes_accessed=12 * rows * width, transcendentals=0
        ),
        name="final",
    )(doc_lengths, x, g, b, c, rates_steps, gains, into, back)

    tokens_all = lax.axis_size("dp") * lax.axis_size("seq") * rows * HEAD_DIM
    return y[None], gx[None], sums / math.sqrt(tokens_all)


def solution(mesh):
    placed = (
        P("dp", "seq", "head"),
        P("dp", "seq", None),
        P("dp", "seq", None),
        P("dp", "head", "seq"),
        P("head"),
        P("dp", None),
        P("dp", ("seq", "head"), None),
    )
    return jax.shard_map(
        shards,
        mesh=mesh,
        in_specs=placed,
        out_specs=(P("dp", "seq", "head"), P("dp", "seq", "head"), P("head")),
        check_vma=False,
    )
```

```python
import functools
import math

import jax
import jax.numpy as jnp
from jax import lax
from jax.experimental import pallas as pl
from jax.experimental.pallas import tpu as pltpu
from jax.sharding import PartitionSpec as P

HEAD_DIM = 64
GROUP = 128
LANES = 128
PAIR = LANES // HEAD_DIM
EXACT = lax.Precision.HIGHEST
F32 = jnp.float32
BF16 = jnp.bfloat16


def split(value, axis):
    high = value.astype(BF16)
    low = (value - high.astype(F32)).astype(BF16)
    return jnp.concatenate([high, low], axis=axis)


def dot(a, b):
    return jnp.dot(a, b, preferred_element_type=F32)


def tdot(a, b):
    return lax.dot_general(a, b, (((0,), (0,)), ((), ())), preferred_element_type=F32)


def ndot(a, b):
    return lax.dot_general(a, b, (((1,), (1,)), ((), ())), preferred_element_type=F32)


def iota(axis):
    return lax.broadcasted_iota(jnp.int32, (GROUP, GROUP), axis)


def doc_of(position, ends):
    return sum((position >= end).astype(jnp.int32) for end in ends)


def doc_ends(lengths_ref):
    ends = []
    total = jnp.int32(0)
    for k in range(lengths_ref.shape[1] - 1):
        total = total + lengths_ref[0, k]
        ends.append(total)
    return ends


def block_masks(ends, first):
    here = doc_of(first + iota(0), ends)
    prev = doc_of(jnp.full((GROUP, GROUP), first - 1, jnp.int32), ends)
    last = doc_of(jnp.full((GROUP, GROUP), first + GROUP - 1, jnp.int32), ends)
    return here, (here == prev).astype(F32), (here == last).astype(F32)


def running_columns(rates, lower):
    return lax.dot_general(
        lower, rates, (((1,), (1,)), ((), ())), precision=EXACT, preferred_element_type=F32
    )


def pair_columns(columns, pair):
    wide = [
        jnp.broadcast_to(columns[:, h : h + 1], (GROUP, GROUP))
        for h in range(pair * PAIR, pair * PAIR + PAIR)
    ]
    lane_head = iota(1) // HEAD_DIM
    joined = wide[0]
    for h in range(1, PAIR):
        joined = jnp.where(lane_head == h, wide[h], joined)
    return wide, joined


LAG = 2


def exchange_kernel(scale, lengths_ref, x_ref, gy_ref, b_ref, c_ref, rates_ref, skip_ref,
                    y_ref, gx_ref, sums_ref,
                    g_ref, into_ref, back_ref, partial_ref, gathered_ref,
                    state_out, adjoint_out, from_mask, to_mask, b_t, c_t, inner_ref, inner_t_ref,
                    send_f, recv_f, send_b, recv_b, send_g, recv_g, send_p, recv_p, own_sem):
    rows, width = x_ref.shape
    blocks = rows // GROUP
    pair_count = width // LANES
    own_rows = gy_ref.shape[0]
    count, me = lax.axis_size("seq"), lax.axis_index("seq")
    head_count, head_me = lax.axis_size("head"), lax.axis_index("head")
    later = jnp.minimum(me + 1, count - 1)
    earlier = jnp.maximum(me - 1, 0)
    first, last = me == 0, me == count - 1
    mesh_id = pl.DeviceIdType.MESH

    own = pltpu.make_async_copy(
        gy_ref.at[:, pl.ds(pl.multiple_of(head_me * width, LANES), width)],
        g_ref.at[pl.ds(pl.multiple_of(head_me * own_rows, own_rows), own_rows)],
        own_sem,
    )
    own.start()
    barrier = pltpu.get_barrier_semaphore()

    copies = lax.axis_size("dp") * count
    copy_me = lax.axis_index("dp") * count + me

    def copy_peer(i):
        other = lax.rem(copy_me + i, copies)
        return {"dp": other // count, "seq": lax.rem(other, count)}

    @pl.loop(1, copies)
    def _(i):
        pl.semaphore_signal(barrier, inc=1, device_id=copy_peer(i), device_id_type=mesh_id)

    @pl.loop(1, head_count)
    def _(i):
        pl.semaphore_signal(
            barrier, inc=1, device_id={"head": lax.rem(head_me + i, head_count)},
            device_id_type=mesh_id)

    pl.semaphore_wait(barrier, head_count - 1 + copies - 1)

    def part(i):
        return pltpu.make_async_remote_copy(
            src_ref=partial_ref, dst_ref=gathered_ref.at[copy_me], send_sem=send_p.at[i - 1],
            recv_sem=recv_p.at[i - 1], device_id=copy_peer(i), device_id_type=mesh_id)

    def lanes_of(q):
        return pl.ds(pl.multiple_of(q * LANES, LANES), LANES)

    def cotangent(i, q):
        peer = lax.rem(head_me + i, head_count)
        return pltpu.make_async_remote_copy(
            src_ref=gy_ref.at[:, pl.ds(pl.multiple_of(peer * width + q * LANES, LANES), LANES)],
            dst_ref=g_ref.at[pl.ds(pl.multiple_of(head_me * own_rows, own_rows), own_rows), lanes_of(q)],
            send_sem=send_g.at[i - 1, q], recv_sem=recv_g.at[i - 1, q],
            device_id={"head": peer}, device_id_type=mesh_id)

    def forward(q):
        return pltpu.make_async_remote_copy(
            src_ref=state_out.at[q], dst_ref=into_ref.at[q], send_sem=send_f.at[q],
            recv_sem=recv_f.at[q], device_id={"seq": later}, device_id_type=mesh_id)

    def backward(q):
        return pltpu.make_async_remote_copy(
            src_ref=adjoint_out.at[q], dst_ref=back_ref.at[q], send_sem=send_b.at[q],
            recv_sem=recv_b.at[q], device_id={"seq": earlier}, device_id_type=mesh_id)

    @pl.loop(0, pair_count)
    def _(q):
        @pl.loop(1, head_count)
        def _(i):
            cotangent(i, q).start()

    ends = doc_ends(lengths_ref)
    for k in range(blocks):
        span = slice(k * GROUP, (k + 1) * GROUP)
        at = me * rows + k * GROUP
        here, from_mask[k], to_mask[k] = block_masks(ends, at)
        across = doc_of(at + iota(1), ends)
        inner = ndot(c_ref[span], b_ref[span])
        inner_ref[k] = jnp.where((here == across) & (iota(0) >= iota(1)), inner, 0.0)
        inner_t = ndot(b_ref[span], c_ref[span])
        inner_t_ref[k] = jnp.where((here == across) & (iota(0) <= iota(1)), inner_t, 0.0)
        bt = b_ref[span].astype(F32).T.astype(BF16)
        ct = c_ref[span].astype(F32).T.astype(BF16)
        b_t[k] = jnp.concatenate([bt, bt], axis=1)
        c_t[k] = jnp.concatenate([ct, ct], axis=1)
    own.wait()
    lower = (iota(1) <= iota(0)).astype(F32)

    upper = (iota(0) <= iota(1)).astype(F32)
    lane_head = iota(1) // HEAD_DIM

    def stack(value):
        zero = jnp.zeros_like(value)
        return jnp.concatenate([jnp.where(lane_head == h, value, zero) for h in range(PAIR)], axis=0)

    def runs_of(q):
        runs = []
        for k in range(blocks):
            rates = rates_ref[q, :, k * GROUP : (k + 1) * GROUP]
            line = jnp.dot(rates, upper, precision=EXACT, preferred_element_type=F32)
            runs.append((line,) + pair_columns(running_columns(rates, lower), 0))
        return runs

    def forward_step(q):
        state = jnp.zeros((b_ref.shape[1], LANES), F32)
        decay = jnp.ones((1, LANES), F32)
        runs = runs_of(q)
        kept = []
        for k, (_, _, run) in enumerate(runs):
            total = run[GROUP - 1 : GROUP]
            go = jnp.exp(run - total) * to_mask[k]
            end = jnp.exp(-total) * from_mask[k, GROUP - 1 : GROUP]
            x = x_ref[k * GROUP : (k + 1) * GROUP, lanes_of(q)].astype(F32)
            add = dot(b_t[k], split(go * x, 0))
            state = end * state + add
            decay = decay * end
            kept.append((end, add))

        @pl.when(first)
        def _():
            into_ref[q] = jnp.zeros_like(state)
            state_out[q] = state
            forward(q).start()

        @pl.when(jnp.logical_not(first))
        def _():
            forward(q).wait_recv()

            @pl.when(jnp.logical_not(last))
            def _():
                state_out[q] = decay * into_ref[q] + state
                forward(q).start()

        state = into_ref[q]
        for k, (line, wide, run) in enumerate(runs):
            span = slice(k * GROUP, (k + 1) * GROUP)
            inner = inner_ref[k]
            scores = jnp.concatenate(
                [(jnp.exp(jnp.minimum(line[h : h + 1] - wide[h], 0.0)) * inner).astype(BF16)
                 for h in range(PAIR)], axis=1)
            x = x_ref[span, lanes_of(q)]
            c = c_ref[span]
            come = jnp.exp(-run) * from_mask[k]
            carried = come * dot(jnp.concatenate([c, c], axis=1), split(state, 0))
            y_ref[span, lanes_of(q)] = (
                dot(scores, stack(x)) + carried + skip_ref[q] * x.astype(F32)
            ).astype(BF16)
            end, add = kept[k]
            state = end * state + add

    def backward_step(q):
        @pl.loop(1, head_count)
        def _(i):
            cotangent(i, q).wait_recv()

        adjoint = jnp.zeros((b_ref.shape[1], LANES), F32)
        decay = jnp.ones((1, LANES), F32)
        partial = jnp.zeros((GROUP, LANES), F32)
        runs = runs_of(q)
        kept = [None] * blocks
        for k in reversed(range(blocks)):
            come = jnp.exp(-runs[k][2]) * from_mask[k]
            end = come[GROUP - 1 : GROUP]
            x = x_ref[k * GROUP : (k + 1) * GROUP, lanes_of(q)].astype(F32)
            g = g_ref[k * GROUP : (k + 1) * GROUP, lanes_of(q)].astype(F32)
            partial = partial + x * g
            add = dot(c_t[k], split(come * g, 0))
            adjoint = end * adjoint + add
            decay = decay * end
            kept[k] = (end, add)
        partial_ref[pl.ds(q, 1)] = jnp.sum(partial, axis=0, keepdims=True)

        @pl.when(last)
        def _():
            back_ref[q] = jnp.zeros_like(adjoint)
            adjoint_out[q] = adjoint
            backward(q).start()

        @pl.when(jnp.logical_not(last))
        def _():
            backward(q).wait_recv()

            @pl.when(jnp.logical_not(first))
            def _():
                adjoint_out[q] = decay * back_ref[q] + adjoint
                backward(q).start()

        adjoint = back_ref[q]
        for k in reversed(range(blocks)):
            span = slice(k * GROUP, (k + 1) * GROUP)
            line, wide, run = runs[k]
            inner = inner_t_ref[k]
            scores = jnp.concatenate(
                [(jnp.exp(jnp.minimum(wide[h] - line[h : h + 1], 0.0)) * inner).astype(BF16)
                 for h in range(PAIR)], axis=1)
            g = g_ref[span, lanes_of(q)]
            b = b_ref[span]
            go = jnp.exp(run - run[GROUP - 1 : GROUP]) * to_mask[k]
            carried = go * dot(jnp.concatenate([b, b], axis=1), split(adjoint, 0))
            gx_ref[span, lanes_of(q)] = (
                dot(scores, stack(g)) + carried + skip_ref[q] * g.astype(F32)
            ).astype(BF16)
            end, add = kept[k]
            adjoint = end * adjoint + add

    @pl.loop(0, pair_count + LAG * (count - 1))
    def _(t):
        q = t - LAG * me
        r = t - LAG * (count - 1 - me)

        @pl.when((q >= 0) & (q < pair_count))
        def _():
            forward_step(q)

        @pl.when((r >= 0) & (r < pair_count))
        def _():
            backward_step(r)

    @pl.loop(1, copies)
    def _(i):
        part(i).start()

    gathered_ref[copy_me] = partial_ref[...]

    @pl.loop(0, pair_count)
    def _(q):
        @pl.loop(1, head_count)
        def _(i):
            cotangent(i, q).wait_send()

        @pl.when(jnp.logical_not(last))
        def _():
            forward(q).wait_send()

        @pl.when(jnp.logical_not(first))
        def _():
            backward(q).wait_send()

    @pl.loop(1, copies)
    def _(i):
        part(i).wait()

    total = gathered_ref[0]
    for other in range(1, copies):
        total = total + gathered_ref[other]
    lane = lax.broadcasted_iota(jnp.int32, total.shape, 1) // HEAD_DIM
    sums_ref[...] = jnp.concatenate(
        [jnp.sum(jnp.where(lane == h, total, 0.0), axis=1, keepdims=True) for h in range(PAIR)],
        axis=1) / scale


def shards(x_in, b_in, c_in, rates, skip, doc_lengths, grad_y):
    _, rows, width = x_in.shape
    heads = skip.shape[0]
    state_dim = b_in.shape[2]
    pairs = width // LANES
    blocks = rows // GROUP
    peers = lax.axis_size("head") - 1
    copies = lax.axis_size("dp") * lax.axis_size("seq")
    tokens_all = copies * rows * HEAD_DIM
    gains = jnp.repeat(skip, HEAD_DIM).reshape(pairs, 1, LANES)
    vmem = pl.BlockSpec(memory_space=pltpu.VMEM)
    dma = pltpu.SemaphoreType.DMA
    shape = jax.ShapeDtypeStruct((rows, width), BF16)
    states = pltpu.VMEM((pairs, state_dim, LANES), F32)
    square = pltpu.VMEM((blocks, GROUP, GROUP), F32)
    twice = pltpu.VMEM((blocks, state_dim, 2 * GROUP), BF16)
    y, gx, sums = pl.pallas_call(
        functools.partial(exchange_kernel, math.sqrt(tokens_all)),
        in_specs=[pl.BlockSpec(memory_space=pltpu.SMEM)] + [vmem] * 6,
        out_specs=[vmem] * 3,
        out_shape=[shape, shape, jax.ShapeDtypeStruct((pairs, PAIR), F32)],
        scratch_shapes=[
            pltpu.VMEM((rows, width), BF16), states, states,
            pltpu.VMEM((pairs, LANES), F32), pltpu.VMEM((copies, pairs, LANES), F32),
            states, states, square, square, twice, twice, square, square,
        ] + [dma((pairs,))] * 4 + [dma((peers, pairs))] * 2 + [dma((copies - 1,))] * 2 + [dma],
        compiler_params=pltpu.CompilerParams(collective_id=0, has_side_effects=True),
        name="exchange",
    )(doc_lengths, x_in[0], grad_y[0], b_in[0], c_in[0], rates.reshape(pairs, PAIR, rows), gains)
    return y[None], gx[None], sums.reshape(heads)


def solution(mesh):
    placed = (
        P("dp", "seq", "head"),
        P("dp", "seq", None),
        P("dp", "seq", None),
        P("dp", "head", "seq"),
        P("head"),
        P("dp", None),
        P("dp", ("seq", "head"), None),
    )
    return jax.shard_map(
        shards,
        mesh=mesh,
        in_specs=placed,
        out_specs=(P("dp", "seq", "head"), P("dp", "seq", "head"), P("head")),
        check_vma=False,
    )
```

```python
import functools
import math

import jax
import jax.numpy as jnp
from jax import lax
from jax.experimental import pallas as pl
from jax.experimental.pallas import tpu as pltpu
from jax.sharding import PartitionSpec as P

HEAD_DIM = 64
GROUP = 128
LANES = 128
PAIR = LANES // HEAD_DIM
EXACT = lax.Precision.HIGHEST
F32 = jnp.float32
BF16 = jnp.bfloat16


def split(value, axis):
    high = value.astype(BF16)
    low = (value - high.astype(F32)).astype(BF16)
    return jnp.concatenate([high, low], axis=axis)


def dot(a, b):
    return jnp.dot(a, b, preferred_element_type=F32)


def tdot(a, b):
    return lax.dot_general(a, b, (((0,), (0,)), ((), ())), preferred_element_type=F32)


def ndot(a, b):
    return lax.dot_general(a, b, (((1,), (1,)), ((), ())), preferred_element_type=F32)


def iota(axis):
    return lax.broadcasted_iota(jnp.int32, (GROUP, GROUP), axis)


def doc_of(position, ends):
    return sum((position >= end).astype(jnp.int32) for end in ends)


def doc_ends(lengths_ref):
    ends = []
    total = jnp.int32(0)
    for k in range(lengths_ref.shape[1] - 1):
        total = total + lengths_ref[0, k]
        ends.append(total)
    return ends


def block_masks(ends, first):
    here = doc_of(first + iota(0), ends)
    prev = doc_of(jnp.full((GROUP, GROUP), first - 1, jnp.int32), ends)
    last = doc_of(jnp.full((GROUP, GROUP), first + GROUP - 1, jnp.int32), ends)
    return here, (here == prev).astype(F32), (here == last).astype(F32)


def running_columns(rates, lower):
    return lax.dot_general(
        lower, rates, (((1,), (1,)), ((), ())), precision=EXACT, preferred_element_type=F32
    )


def pair_columns(columns, pair):
    wide = [
        jnp.broadcast_to(columns[:, h : h + 1], (GROUP, GROUP))
        for h in range(pair * PAIR, pair * PAIR + PAIR)
    ]
    lane_head = iota(1) // HEAD_DIM
    joined = wide[0]
    for h in range(1, PAIR):
        joined = jnp.where(lane_head == h, wide[h], joined)
    return wide, joined


LAG = 3


def exchange_kernel(scale, lengths_ref, x_ref, gy_ref, b_ref, c_ref, rates_ref, skip_ref,
                    y_ref, gx_ref, sums_ref,
                    g_ref, into_ref, back_ref, partial_ref, gathered_ref,
                    state_out, adjoint_out, from_mask, to_mask, b_t, c_t, inner_ref, inner_t_ref,
                    lines_ref, columns_ref,
                    send_f, recv_f, send_b, recv_b, send_g, recv_g, send_p, recv_p, own_sem):
    rows, width = x_ref.shape
    blocks = rows // GROUP
    pair_count = width // LANES
    own_rows = gy_ref.shape[0]
    count, me = lax.axis_size("seq"), lax.axis_index("seq")
    head_count, head_me = lax.axis_size("head"), lax.axis_index("head")
    later = jnp.minimum(me + 1, count - 1)
    earlier = jnp.maximum(me - 1, 0)
    first, last = me == 0, me == count - 1
    mesh_id = pl.DeviceIdType.MESH

    own = pltpu.make_async_copy(
        gy_ref.at[:, pl.ds(pl.multiple_of(head_me * width, LANES), width)],
        g_ref.at[pl.ds(pl.multiple_of(head_me * own_rows, own_rows), own_rows)],
        own_sem,
    )
    own.start()
    barrier = pltpu.get_barrier_semaphore()

    copies = lax.axis_size("dp") * count
    copy_me = lax.axis_index("dp") * count + me

    def copy_peer(i):
        other = lax.rem(copy_me + i, copies)
        return {"dp": other // count, "seq": lax.rem(other, count)}

    @pl.loop(1, copies)
    def _(i):
        pl.semaphore_signal(barrier, inc=1, device_id=copy_peer(i), device_id_type=mesh_id)

    @pl.loop(1, head_count)
    def _(i):
        pl.semaphore_signal(
            barrier, inc=1, device_id={"head": lax.rem(head_me + i, head_count)},
            device_id_type=mesh_id)

    pl.semaphore_wait(barrier, head_count - 1 + copies - 1)

    def part(i):
        return pltpu.make_async_remote_copy(
            src_ref=partial_ref, dst_ref=gathered_ref.at[copy_me], send_sem=send_p.at[i - 1],
            recv_sem=recv_p.at[i - 1], device_id=copy_peer(i), device_id_type=mesh_id)

    def lanes_of(q):
        return pl.ds(pl.multiple_of(q * LANES, LANES), LANES)

    def cotangent(i, q):
        peer = lax.rem(head_me + i, head_count)
        return pltpu.make_async_remote_copy(
            src_ref=gy_ref.at[:, pl.ds(pl.multiple_of(peer * width + q * LANES, LANES), LANES)],
            dst_ref=g_ref.at[pl.ds(pl.multiple_of(head_me * own_rows, own_rows), own_rows), lanes_of(q)],
            send_sem=send_g.at[i - 1, q], recv_sem=recv_g.at[i - 1, q],
            device_id={"head": peer}, device_id_type=mesh_id)

    def forward(q):
        return pltpu.make_async_remote_copy(
            src_ref=state_out.at[q], dst_ref=into_ref.at[q], send_sem=send_f.at[q],
            recv_sem=recv_f.at[q], device_id={"seq": later}, device_id_type=mesh_id)

    def backward(q):
        return pltpu.make_async_remote_copy(
            src_ref=adjoint_out.at[q], dst_ref=back_ref.at[q], send_sem=send_b.at[q],
            recv_sem=recv_b.at[q], device_id={"seq": earlier}, device_id_type=mesh_id)

    @pl.loop(0, pair_count)
    def _(q):
        @pl.loop(1, head_count)
        def _(i):
            cotangent(i, q).start()

    ends = doc_ends(lengths_ref)
    for k in range(blocks):
        span = slice(k * GROUP, (k + 1) * GROUP)
        at = me * rows + k * GROUP
        here, from_mask[k], to_mask[k] = block_masks(ends, at)
        across = doc_of(at + iota(1), ends)
        inner = ndot(c_ref[span], b_ref[span])
        inner_ref[k] = jnp.where((here == across) & (iota(0) >= iota(1)), inner, 0.0)
        inner_t = ndot(b_ref[span], c_ref[span])
        inner_t_ref[k] = jnp.where((here == across) & (iota(0) <= iota(1)), inner_t, 0.0)
        bt = b_ref[span].astype(F32).T.astype(BF16)
        ct = c_ref[span].astype(F32).T.astype(BF16)
        b_t[k] = jnp.concatenate([bt, bt], axis=1)
        c_t[k] = jnp.concatenate([ct, ct], axis=1)
    own.wait()
    lower = (iota(1) <= iota(0)).astype(F32)

    upper = (iota(0) <= iota(1)).astype(F32)
    lane_head = iota(1) // HEAD_DIM

    def stack(value):
        zero = jnp.zeros_like(value)
        return jnp.concatenate([jnp.where(lane_head == h, value, zero) for h in range(PAIR)], axis=0)

    for k in range(blocks):
        span = slice(k * GROUP, (k + 1) * GROUP)
        rates = rates_ref[:, span]
        lines = jnp.dot(rates, upper, precision=EXACT, preferred_element_type=F32)
        columns = running_columns(rates, lower)
        for pair in range(pair_count):
            heads = slice(pair * PAIR, (pair + 1) * PAIR)
            lines_ref[pair, :, span] = lines[heads]
            columns_ref[pair, span] = columns[:, heads]

    def runs_of(q):
        runs = []
        for k in range(blocks):
            span = slice(k * GROUP, (k + 1) * GROUP)
            runs.append((lines_ref[q, :, span],) + pair_columns(columns_ref[q, span], 0))
        return runs

    def gain_of(q):
        gain = jnp.full((GROUP, LANES), skip_ref[q * PAIR], F32)
        for h in range(1, PAIR):
            gain = jnp.where(lane_head == h, skip_ref[q * PAIR + h], gain)
        return gain

    def forward_step(q):
        state = jnp.zeros((b_ref.shape[1], LANES), F32)
        decay = jnp.ones((1, LANES), F32)
        runs = runs_of(q)
        kept = []
        for k, (_, _, run) in enumerate(runs):
            total = run[GROUP - 1 : GROUP]
            go = jnp.exp(run - total) * to_mask[k]
            end = jnp.exp(-total) * from_mask[k, GROUP - 1 : GROUP]
            x = x_ref[k * GROUP : (k + 1) * GROUP, lanes_of(q)].astype(F32)
            add = dot(b_t[k], split(go * x, 0))
            state = end * state + add
            decay = decay * end
            kept.append((end, add))

        @pl.when(first)
        def _():
            into_ref[q] = jnp.zeros_like(state)
            state_out[q] = state
            forward(q).start()

        @pl.when(jnp.logical_not(first))
        def _():
            forward(q).wait_recv()

            @pl.when(jnp.logical_not(last))
            def _():
                state_out[q] = decay * into_ref[q] + state
                forward(q).start()

        state = into_ref[q]
        gain = gain_of(q)
        for k, (line, wide, run) in enumerate(runs):
            span = slice(k * GROUP, (k + 1) * GROUP)
            inner = inner_ref[k]
            scores = jnp.concatenate(
                [(jnp.exp(jnp.minimum(line[h : h + 1] - wide[h], 0.0)) * inner).astype(BF16)
                 for h in range(PAIR)], axis=1)
            x = x_ref[span, lanes_of(q)]
            c = c_ref[span]
            come = jnp.exp(-run) * from_mask[k]
            carried = come * dot(jnp.concatenate([c, c], axis=1), split(state, 0))
            y_ref[span, lanes_of(q)] = (
                dot(scores, stack(x)) + carried + gain * x.astype(F32)
            ).astype(BF16)
            end, add = kept[k]
            state = end * state + add

    def backward_step(q):
        @pl.loop(1, head_count)
        def _(i):
            cotangent(i, q).wait_recv()

        adjoint = jnp.zeros((b_ref.shape[1], LANES), F32)
        decay = jnp.ones((1, LANES), F32)
        partial = jnp.zeros((GROUP, LANES), F32)
        runs = runs_of(q)
        kept = [None] * blocks
        for k in reversed(range(blocks)):
            come = jnp.exp(-runs[k][2]) * from_mask[k]
            end = come[GROUP - 1 : GROUP]
            x = x_ref[k * GROUP : (k + 1) * GROUP, lanes_of(q)].astype(F32)
            g = g_ref[k * GROUP : (k + 1) * GROUP, lanes_of(q)].astype(F32)
            partial = partial + x * g
            add = dot(c_t[k], split(come * g, 0))
            adjoint = end * adjoint + add
            decay = decay * end
            kept[k] = (end, add)
        partial_ref[pl.ds(q, 1)] = jnp.sum(partial, axis=0, keepdims=True)

        @pl.when(last)
        def _():
            back_ref[q] = jnp.zeros_like(adjoint)
            adjoint_out[q] = adjoint
            backward(q).start()

        @pl.when(jnp.logical_not(last))
        def _():
            backward(q).wait_recv()

            @pl.when(jnp.logical_not(first))
            def _():
                adjoint_out[q] = decay * back_ref[q] + adjoint
                backward(q).start()

        adjoint = back_ref[q]
        gain = gain_of(q)
        for k in reversed(range(blocks)):
            span = slice(k * GROUP, (k + 1) * GROUP)
            line, wide, run = runs[k]
            inner = inner_t_ref[k]
            scores = jnp.concatenate(
                [(jnp.exp(jnp.minimum(wide[h] - line[h : h + 1], 0.0)) * inner).astype(BF16)
                 for h in range(PAIR)], axis=1)
            g = g_ref[span, lanes_of(q)]
            b = b_ref[span]
            go = jnp.exp(run - run[GROUP - 1 : GROUP]) * to_mask[k]
            carried = go * dot(jnp.concatenate([b, b], axis=1), split(adjoint, 0))
            gx_ref[span, lanes_of(q)] = (
                dot(scores, stack(g)) + carried + gain * g.astype(F32)
            ).astype(BF16)
            end, add = kept[k]
            adjoint = end * adjoint + add

    @pl.loop(0, pair_count + LAG * (count - 1))
    def _(t):
        q = t - LAG * me
        r = t - LAG * (count - 1 - me)

        @pl.when((q >= 0) & (q < pair_count))
        def _():
            forward_step(q)

        @pl.when((r >= 0) & (r < pair_count))
        def _():
            backward_step(r)

    @pl.loop(1, copies)
    def _(i):
        part(i).start()

    gathered_ref[copy_me] = partial_ref[...]

    @pl.loop(0, pair_count)
    def _(q):
        @pl.loop(1, head_count)
        def _(i):
            cotangent(i, q).wait_send()

        @pl.when(jnp.logical_not(last))
        def _():
            forward(q).wait_send()

        @pl.when(jnp.logical_not(first))
        def _():
            backward(q).wait_send()

    @pl.loop(1, copies)
    def _(i):
        part(i).wait()

    total = gathered_ref[0]
    for other in range(1, copies):
        total = total + gathered_ref[other]
    lane = lax.broadcasted_iota(jnp.int32, total.shape, 1) // HEAD_DIM
    sums_ref[...] = jnp.concatenate(
        [jnp.sum(jnp.where(lane == h, total, 0.0), axis=1, keepdims=True) for h in range(PAIR)],
        axis=1) / scale


def shards(x_in, b_in, c_in, rates, skip, doc_lengths, grad_y):
    _, rows, width = x_in.shape
    heads = skip.shape[0]
    state_dim = b_in.shape[2]
    pairs = width // LANES
    blocks = rows // GROUP
    peers = lax.axis_size("head") - 1
    copies = lax.axis_size("dp") * lax.axis_size("seq")
    tokens_all = copies * rows * HEAD_DIM
    smem = pl.BlockSpec(memory_space=pltpu.SMEM)
    vmem = pl.BlockSpec(memory_space=pltpu.VMEM)
    dma = pltpu.SemaphoreType.DMA
    shape = jax.ShapeDtypeStruct((rows, width), BF16)
    states = pltpu.VMEM((pairs, state_dim, LANES), F32)
    square = pltpu.VMEM((blocks, GROUP, GROUP), F32)
    twice = pltpu.VMEM((blocks, state_dim, 2 * GROUP), BF16)
    y, gx, sums = pl.pallas_call(
        functools.partial(exchange_kernel, math.sqrt(tokens_all)),
        in_specs=[smem] + [vmem] * 5 + [smem],
        out_specs=[vmem] * 3,
        out_shape=[shape, shape, jax.ShapeDtypeStruct((pairs, PAIR), F32)],
        scratch_shapes=[
            pltpu.VMEM((rows, width), BF16), states, states,
            pltpu.VMEM((pairs, LANES), F32), pltpu.VMEM((copies, pairs, LANES), F32),
            states, states, square, square, twice, twice, square, square,
            pltpu.VMEM((pairs, PAIR, rows), F32), pltpu.VMEM((pairs, rows, PAIR), F32),
        ] + [dma((pairs,))] * 4 + [dma((peers, pairs))] * 2 + [dma((copies - 1,))] * 2 + [dma],
        compiler_params=pltpu.CompilerParams(collective_id=0, has_side_effects=True),
        name="exchange",
    )(doc_lengths, x_in[0], grad_y[0], b_in[0], c_in[0], rates[0], skip)
    return y[None], gx[None], sums.reshape(heads)


def solution(mesh):
    placed = (
        P("dp", "seq", "head"),
        P("dp", "seq", None),
        P("dp", "seq", None),
        P("dp", "head", "seq"),
        P("head"),
        P("dp", None),
        P("dp", ("seq", "head"), None),
    )
    return jax.shard_map(
        shards,
        mesh=mesh,
        in_specs=placed,
        out_specs=(P("dp", "seq", "head"), P("dp", "seq", "head"), P("head")),
        check_vma=False,
    )
```
